32 devices in a mesh: grp: 2 (over x), reg: 16 (over z, y, core).
Axes of the slice: x: 2, y: 2, z: 4, core: 2. Of those that a mesh axis runs over, the one named last changes fastest.
Arguments:
- waveforms: bfloat16 [32, 3, 4096], P('grp', None, 'reg'), parts along dimension 0, may hold values from -6 to 6
- tail: bfloat16 [32, 3, 768], P('grp'), parts along dimension 0, may hold values from -6 to 6
- station_lists: int32 [32, 4], P('grp'), parts along dimension 0, may hold values from 0 to 15
- station_count: int32 [32], P(('grp', 'reg')), parts along dimension 0, may hold values from 1 to 4, 48 in all
- bank_of_region: int32 [32], P(('grp', 'reg')), parts along dimension 0, may hold values from 0 to 7
- library: bfloat16 [8, 16, 12, 512], replicated, may hold values from -0.25 to 0.25
- moveouts: int32 [32, 16, 12], P(('grp', 'reg')), parts along dimension 0, may hold values from 0 to 2
Outputs:
- detection: float32 [32, 4096], P('grp', 'reg'), parts along dimension 0
The draws below stay inside these ranges and needn't reach their ends.
There are 2 independent parts, one for each index of `grp`. The reference program is written for one: setup_inputs(seed, part) draws one part's arguments, and reference() takes and returns one part's arrays. A program takes and returns all parts, laid end to end along the dimension named above; an argument that names none is the same for every part. Nothing has to cross between parts.
All inputs are finite; a program needn't handle non-finite values. No bound on the sum of `station_count` on one device may be relied on, other than what follows from the above.
Results may differ from the reference program's by a relative error of at most 0.0003.
Values may be sent and summed in bfloat16 or wider, within the bound.
A program may use at most 64 MiB of HBM per device.

```python
import math
import jax
import jax.numpy as jnp
import numpy as np
from jax import lax

TAPS = 512
TEMPLATES = 16
SLOTS = 4
COMPS = 3
BANKS = 8
UNIT = 128
MOVE = 256
REGIONS = 16
STATIONS = 16
LENGTH = 4096
MARGIN = 768


def with_ends(drawn, rng, least, high):
    shape = drawn.shape
    spot = [jax.random.randint(jax.random.fold_in(rng, axis), (), 0, shape[axis]) for axis in range(len(shape))]
    drawn = drawn.at[tuple(spot)].set(least)
    longest = shape.index(max(shape))
    spot[longest] = (spot[longest] + 1) % shape[longest]
    return drawn.at[tuple(spot)].set(high)


def block_scale(own_key, extent, split, low, largest):
    gain = 1.0
    for axis_at, blocks in split:
        steps = jax.random.uniform(jax.random.fold_in(jax.random.fold_in(own_key, 6), axis_at), (blocks,), jnp.float32, low / len(split), largest / len(split))
        gain = gain * jnp.repeat(jnp.exp(steps), extent[axis_at] // blocks).reshape((-1,) + (1,) * (len(extent) - 1 - axis_at))
    return gain


def split_up(number_of, total, reach, lean):
    portions = [(1 << 20) // math.isqrt(grade ** lean) + 1 for grade in range(2, number_of + 1)]
    rest, holding = total - reach - (number_of - 1), [1] * (number_of - 1)
    while rest > 0:
        candidates = [i for i in range(number_of - 1) if holding[i] < reach]
        mass, remaining = sum([portions[i] for i in candidates]), rest
        for i in candidates:
            extra = min(reach - holding[i], max(1, remaining * portions[i] // mass), rest)
            holding[i] = holding[i] + extra
            rest = rest - extra
    return np.array([reach] + holding)


def ragged(own_key, number_of, total, most, lean):
    if number_of == 2:
        one = jax.random.randint(own_key, (), max(1, total - most), min(most, total - 1) + 1)
        return jnp.stack([one, total - one])
    tallies = jnp.asarray(split_up(number_of, total, most, lean), jnp.int32)
    twos = (number_of - 1) // 2
    giver, taker = tallies[1:1 + 2 * twos:2], tallies[2:2 + 2 * twos:2]
    margin = jnp.minimum(giver - 1, most - taker)
    passed = jax.random.randint(jax.random.fold_in(own_key, 1), (twos,), 0, 1 << 20) % (margin + 1)
    tallies = tallies.at[1:1 + 2 * twos:2].set(giver - passed).at[2:2 + 2 * twos:2].set(taker + passed)
    return tallies[jax.random.permutation(jax.random.fold_in(own_key, 2), number_of)]


def scatter_about(rng, extent, width, reach, shards=(), kind=jnp.bfloat16):
    level = block_scale(rng, extent, shards, -0.22, 0.18) if shards else 1.0
    array = jax.random.normal(rng, extent, jnp.float32) * width * level
    return jnp.minimum(jnp.maximum(array, -reach), reach).astype(kind)


def setup_inputs(seed: int = 0, part: int = 0) -> dict:
    keys = jax.random.split(jax.random.key(seed), 8)
    own_keys = jax.random.split(jax.random.fold_in(keys[7], part), 8)
    waveforms = scatter_about(own_keys[0], (STATIONS, COMPS, LENGTH), 1.0, 6.0, ((2, 16),))
    tail = scatter_about(own_keys[1], (STATIONS, COMPS, MARGIN), 1.0, 6.0)
    station_lists = with_ends(jax.random.randint(own_keys[2], (REGIONS, SLOTS), 0, STATIONS), jax.random.fold_in(own_keys[2], 1), 0, STATIONS - 1).astype(jnp.int32)
    station_count = ragged(own_keys[3], REGIONS, (SLOTS - 1) * REGIONS, SLOTS, 2).astype(jnp.int32)
    bank_of_region = with_ends(jax.random.randint(own_keys[4], (REGIONS,), 0, BANKS), jax.random.fold_in(own_keys[4], 1), 0, BANKS - 1).astype(jnp.int32)
    library = scatter_about(keys[5], (BANKS, TEMPLATES, SLOTS * COMPS, TAPS), TAPS ** -0.5, 0.25)
    moveouts = with_ends(jax.random.randint(own_keys[6], (REGIONS, TEMPLATES, SLOTS * COMPS), 0, MOVE // UNIT + 1), jax.random.fold_in(own_keys[6], 1), 0, (MOVE // UNIT + 1) - 1).astype(jnp.int32)
    return dict(waveforms=waveforms, tail=tail, station_lists=station_lists, station_count=station_count, bank_of_region=bank_of_region, library=library, moveouts=moveouts)


def reference(waveforms, tail, station_lists, station_count, bank_of_region, library, moveouts):
    complete = jnp.concatenate([waveforms, tail], axis=2)
    record_len = LENGTH + MARGIN
    out_len = LENGTH + MOVE
    fft_size = 1 << (record_len + TAPS).bit_length()
    channels = SLOTS * COMPS
    positions = jnp.arange(LENGTH, dtype=jnp.int32)

    def add_region(running, region):
        station_ids = lax.dynamic_index_in_dim(station_lists, region, 0, keepdims=False)
        signal = complete[station_ids].reshape(channels, record_len).astype(jnp.float32)
        bank_id = lax.dynamic_index_in_dim(bank_of_region, region, 0, keepdims=False)
        kernels = lax.dynamic_index_in_dim(library, bank_id, 0, keepdims=False).astype(jnp.float32)
        spectrum = jnp.fft.rfft(signal, fft_size)
        kernel_spec = jnp.fft.rfft(kernels, fft_size)
        correlation = jnp.fft.irfft(spectrum[None] * jnp.conj(kernel_spec), fft_size)[:, :, :out_len]
        squares = signal * signal
        cumulative = jnp.concatenate([jnp.zeros((channels, 1), squares.dtype), jnp.cumsum(squares, axis=1)], axis=1)
        energy = cumulative[:, TAPS:TAPS + out_len] - cumulative[:, :out_len]
        scaled = correlation / jnp.sqrt(energy / TAPS + 1e-05)[None]
        shifts = lax.dynamic_index_in_dim(moveouts, region, 0, keepdims=False)
        index = (shifts * UNIT).astype(jnp.int32)[:, :, None] + positions[None, None, :]
        shifted = jnp.take_along_axis(scaled, index, axis=2)
        count = lax.dynamic_index_in_dim(station_count, region, 0, keepdims=False)
        live_mask = (jnp.arange(channels, dtype=jnp.int32) // COMPS < count).astype(scaled.dtype)
        return (running + lax.optimization_barrier(jnp.sum(shifted * live_mask[None, :, None], axis=1)), None)
    start = jnp.zeros((TEMPLATES, LENGTH), jnp.float32)
    total, unused = lax.scan(add_region, start, jnp.arange(REGIONS, dtype=jnp.int32))
    return total / jnp.sqrt(jnp.float32(COMPS * SLOTS * REGIONS))
```

```python
import functools
import math

import jax
import jax.numpy as jnp
from jax import lax
from jax.experimental import pallas as pl
from jax.experimental.pallas import tpu as pltpu
from jax.sharding import PartitionSpec as P

UNIT = 128
PAIRS = 4


def exchange_kernel(n, wave_ref, tail_ref, mov_ref, count_ref, bank_ref, rec_ref, meta_ref,
                    mine, halo_send, halo_recv, meta_send, meta_recv):
    me = lax.axis_index("reg")
    piece = wave_ref.shape[2]
    halos = tail_ref.shape[2] // piece
    channels = mov_ref.shape[2]

    mine[...] = jnp.zeros_like(mine)
    mine[:, 0:channels] = mov_ref[0]
    mine[:, channels:channels + 1] = jnp.full((mine.shape[0], 1), count_ref[0], jnp.int32)
    mine[:, channels + 1:channels + 2] = jnp.full((mine.shape[0], 1), bank_ref[0], jnp.int32)

    barrier = pltpu.get_barrier_semaphore()

    @pl.loop(1, n)
    def _(step):
        pl.semaphore_signal(barrier, inc=1, device_id={"reg": lax.rem(me + step, n)},
                            device_id_type=pl.DeviceIdType.MESH)

    pl.semaphore_wait(barrier, n - 1)

    def halo_copy(h):
        return pltpu.make_async_remote_copy(
            src_ref=wave_ref,
            dst_ref=rec_ref.at[:, :, pl.ds(h * piece, piece)],
            send_sem=halo_send.at[h - 1],
            recv_sem=halo_recv.at[h - 1],
            device_id={"reg": lax.rem(me + n - h, n)},
            device_id_type=pl.DeviceIdType.MESH,
        )

    for h in range(1, halos + 1):
        @pl.when(me >= h)
        def _():
            halo_copy(h).start()

    def meta_copy(step):
        return pltpu.make_async_remote_copy(
            src_ref=mine,
            dst_ref=meta_ref.at[me],
            send_sem=meta_send.at[step],
            recv_sem=meta_recv.at[step],
            device_id={"reg": lax.rem(me + step, n)},
            device_id_type=pl.DeviceIdType.MESH,
        )

    @pl.loop(1, n)
    def _(step):
        meta_copy(step).start()

    meta_ref[me] = mine[...]
    rec_ref[:, :, 0:piece] = wave_ref[...]
    for h in range(1, halos + 1):
        for q in range(h):
            @pl.when(me + h - n == q)
            def _():
                rec_ref[:, :, h * piece:(h + 1) * piece] = tail_ref[:, :, q * piece:(q + 1) * piece]

    for h in range(1, halos + 1):
        @pl.when(me >= h)
        def _():
            halo_copy(h).wait_send()

        @pl.when(me + h < n)
        def _():
            halo_copy(h).wait_recv()

    @pl.loop(1, n)
    def _(step):
        meta_copy(step).wait_send()
        meta_copy(step).wait_recv()


def exchange(n, waveforms, tail, moveouts, station_count, bank_of_region):
    stations, comps, piece = waveforms.shape
    templates = moveouts.shape[1]
    halos = tail.shape[2] // piece
    vmem = pl.BlockSpec(memory_space=pltpu.VMEM)
    smem = pl.BlockSpec(memory_space=pltpu.SMEM)
    return pl.pallas_call(
        functools.partial(exchange_kernel, n),
        out_shape=(
            jax.ShapeDtypeStruct((stations, comps, piece + tail.shape[2]), waveforms.dtype),
            jax.ShapeDtypeStruct((n, templates, 128), jnp.int32),
        ),
        in_specs=[vmem, vmem, vmem, smem, smem],
        out_specs=(vmem, vmem),
        scratch_shapes=[
            pltpu.VMEM((templates, 128), jnp.int32),
            pltpu.SemaphoreType.DMA((halos,)),
            pltpu.SemaphoreType.DMA((halos,)),
            pltpu.SemaphoreType.DMA((n,)),
            pltpu.SemaphoreType.DMA((n,)),
        ],
        compiler_params=pltpu.CompilerParams(collective_id=0, has_side_effects=True,
                                             vmem_limit_bytes=32 << 20),
        name="exchange",
    )(waveforms, tail, moveouts, station_count, bank_of_region)


def stack_kernel(comps, taps, piece, scale, lists_ref, scal_ref, rec_ref, lib_ref, mov_ref, out_ref,
                 hank, gain, pairs, place):
    stations, _, record = rec_ref.shape
    regions, slots = lists_ref.shape
    channels = slots * comps
    templates = lib_ref.shape[1]
    moves = (record - piece - taps) // UNIT + 1
    width = piece + (moves - 1) * UNIT
    deep = 2 * UNIT
    reach = width + taps - deep

    @pl.loop(0, stations + 1)
    def _(s):
        place[s] = 0

    @pl.loop(0, regions)
    def _(r):
        @pl.loop(0, scal_ref[r, 0])
        def _(k):
            s = lists_ref[r, k]
            place[s + 1] = place[s + 1] + 1

    @pl.loop(0, stations)
    def _(s):
        place[s + 1] = place[s + 1] + place[s]

    @pl.loop(0, regions)
    def _(r):
        @pl.loop(0, scal_ref[r, 0])
        def _(k):
            s = lists_ref[r, k]
            pairs[place[s]] = r * slots + k
            place[s] = place[s] + 1

    out_ref[...] = jnp.zeros_like(out_ref)
    sub = lax.broadcasted_iota(jnp.int32, (8, record), 0)
    lane = lax.broadcasted_iota(jnp.int32, (templates, UNIT), 1)

    @pl.loop(0, stations)
    def _(s):
        end = place[s]
        begin = jnp.where(s == 0, 0, place[jnp.maximum(s - 1, 0)])

        @pl.when(end > begin)
        def _():
            x = rec_ref[s].astype(jnp.float32)
            window = x * x
            span = 1
            while span < taps:
                window = window + pltpu.roll(window, record - span, 1)
                span *= 2
            gain[...] = lax.rsqrt(window[:, 0:width] / taps + 1e-05) * scale
            for c in range(comps):
                fan = jnp.broadcast_to(x[c:c + 1], (8, record))
                for bit in (1, 2, 4):
                    fan = jnp.where(sub & bit != 0, pltpu.roll(fan, record - bit, 1), fan)
                for g in range(0, UNIT, 16):
                    low = pltpu.roll(fan, record - g, 1) if g else fan
                    both = jnp.concatenate([low, pltpu.roll(fan, record - g - 8, 1)], axis=0)
                    both = both.astype(jnp.bfloat16)
                    hank[c, g:g + 16] = both[:, 0:reach]
                    hank[c, UNIT + g:UNIT + g + 16] = both[:, UNIT:UNIT + reach]

            @pl.loop(0, pl.cdiv(end - begin, PAIRS))
            def _(q):
                first = begin + q * PAIRS
                picks = []
                for p in range(PAIRS):
                    at = jnp.minimum(first + p, end - 1)
                    pair = pairs[at]
                    r = pair // slots
                    slot = pair - r * slots
                    picks.append((r, scal_ref[r, 1] * channels + slot * comps, slot * comps,
                                  jnp.where(first + p < end, 0, moves)))
                total = jnp.zeros(out_ref.shape, jnp.float32)
                for c in range(comps):
                    rows = jnp.concatenate([lib_ref[base + c] for _, base, _, _ in picks], axis=0)
                    corr = None
                    for d in range(taps // deep):
                        term = jnp.dot(rows[:, d * deep:(d + 1) * deep],
                                       hank[c, :, d * deep:d * deep + width],
                                       preferred_element_type=jnp.float32)
                        corr = term if corr is None else corr + term
                    corr = corr * gain[c:c + 1, :]
                    for p, (r, _, channel, dead) in enumerate(picks):
                        mine = corr[p * templates:(p + 1) * templates]
                        shift = jnp.sum(jnp.where(lane == channel + c, mov_ref[r], 0), axis=1,
                                        keepdims=True) + dead
                        for m in range(moves):
                            total = total + jnp.where(shift == m, mine[:, m * UNIT:m * UNIT + piece], 0.0)
                out_ref[...] += total


def stack(comps, taps, piece, scale, lists, scal, record, bank_rows, meta):
    regions, slots = lists.shape
    stations = record.shape[0]
    templates = bank_rows.shape[1]
    width = record.shape[2] - taps
    vmem = pl.BlockSpec(memory_space=pltpu.VMEM)
    smem = pl.BlockSpec(memory_space=pltpu.SMEM)
    return pl.pallas_call(
        functools.partial(stack_kernel, comps, taps, piece, scale),
        out_shape=jax.ShapeDtypeStruct((templates, piece), jnp.float32),
        in_specs=[smem, smem, vmem, vmem, vmem],
        out_specs=vmem,
        scratch_shapes=[
            pltpu.VMEM((comps, 2 * UNIT, width + taps - 2 * UNIT), jnp.bfloat16),
            pltpu.VMEM((comps, width), jnp.float32),
            pltpu.SMEM((regions * slots,), jnp.int32),
            pltpu.SMEM((stations + 1,), jnp.int32),
        ],
        compiler_params=pltpu.CompilerParams(vmem_limit_bytes=32 << 20),
        name="stack",
    )(lists, scal, record, bank_rows, meta)


def on_device(waveforms, tail, station_lists, station_count, bank_of_region, library, moveouts):
    regions = lax.axis_size("reg")
    comps, piece = waveforms.shape[1:]
    banks, templates, channels, taps = library.shape
    slots = station_lists.shape[1]
    scale = 1.0 / math.sqrt(comps * slots * regions)
    bank_rows = jnp.transpose(library, (0, 2, 1, 3)).reshape(banks * channels, templates, taps)
    record, meta = exchange(regions, waveforms, tail, moveouts, station_count, bank_of_region)
    scal = meta[:, 0, channels:channels + 2]
    return stack(comps, taps, piece, scale, station_lists, scal, record, bank_rows, meta)


def solution(mesh):
    return jax.shard_map(
        on_device,
        mesh=mesh,
        in_specs=(
            P("grp", None, "reg"),
            P("grp", None, None),
            P("grp", None),
            P(("grp", "reg")),
            P(("grp", "reg")),
            P(),
            P(("grp", "reg"), None, None),
        ),
        out_specs=P("grp", "reg"),
        check_vma=False,
    )
```

```python
import functools
import math

import jax
import jax.numpy as jnp
from jax import lax
from jax.experimental import pallas as pl
from jax.experimental.pallas import tpu as pltpu
from jax.sharding import PartitionSpec as P

UNIT = 128
PAIRS = 4


def exchange_kernel(n, wave_ref, tail_ref, mov_ref, count_ref, bank_ref, rec_ref, meta_ref,
                    mine, halo_send, halo_recv, meta_send, meta_recv):
    me = lax.axis_index("reg")
    piece = wave_ref.shape[2]
    halos = tail_ref.shape[2] // piece
    channels, _, templates = mov_ref.shape

    mine[...] = jnp.zeros_like(mine)
    for c in range(channels):
        mine[c:c + 1, 0:templates] = mov_ref[c]
    mine[channels:channels + 1] = jnp.full((1, mine.shape[1]), count_ref[0], jnp.int32)
    mine[channels + 1:channels + 2] = jnp.full((1, mine.shape[1]), bank_ref[0], jnp.int32)

    barrier = pltpu.get_barrier_semaphore()

    @pl.loop(1, n)
    def _(step):
        pl.semaphore_signal(barrier, inc=1, device_id={"reg": lax.rem(me + step, n)},
                            device_id_type=pl.DeviceIdType.MESH)

    pl.semaphore_wait(barrier, n - 1)

    def halo_copy(h):
        return pltpu.make_async_remote_copy(
            src_ref=wave_ref,
            dst_ref=rec_ref.at[:, :, pl.ds(h * piece, piece)],
            send_sem=halo_send.at[h - 1],
            recv_sem=halo_recv.at[h - 1],
            device_id={"reg": lax.rem(me + n - h, n)},
            device_id_type=pl.DeviceIdType.MESH,
        )

    for h in range(1, halos + 1):
        @pl.when(me >= h)
        def _():
            halo_copy(h).start()

    def meta_copy(step):
        return pltpu.make_async_remote_copy(
            src_ref=mine,
            dst_ref=meta_ref.at[me],
            send_sem=meta_send.at[step],
            recv_sem=meta_recv.at[step],
            device_id={"reg": lax.rem(me + step, n)},
            device_id_type=pl.DeviceIdType.MESH,
        )

    @pl.loop(1, n)
    def _(step):
        meta_copy(step).start()

    meta_ref[me] = mine[...]
    rec_ref[:, :, 0:piece] = wave_ref[...]
    for h in range(1, halos + 1):
        for q in range(h):
            @pl.when(me + h - n == q)
            def _():
                rec_ref[:, :, h * piece:(h + 1) * piece] = tail_ref[:, :, q * piece:(q + 1) * piece]

    for h in range(1, halos + 1):
        @pl.when(me >= h)
        def _():
            halo_copy(h).wait_send()

        @pl.when(me + h < n)
        def _():
            halo_copy(h).wait_recv()

    @pl.loop(1, n)
    def _(step):
        meta_copy(step).wait_send()
        meta_copy(step).wait_recv()


def exchange(n, waveforms, tail, moveouts, station_count, bank_of_region):
    comps, stations, piece = waveforms.shape
    height = -(-(moveouts.shape[0] + 2) // 8) * 8
    halos = tail.shape[2] // piece
    vmem = pl.BlockSpec(memory_space=pltpu.VMEM)
    smem = pl.BlockSpec(memory_space=pltpu.SMEM)
    return pl.pallas_call(
        functools.partial(exchange_kernel, n),
        out_shape=(
            jax.ShapeDtypeStruct((comps, stations, piece + tail.shape[2]), waveforms.dtype),
            jax.ShapeDtypeStruct((n, height, 128), jnp.int32),
        ),
        in_specs=[vmem, vmem, vmem, smem, smem],
        out_specs=(vmem, vmem),
        scratch_shapes=[
            pltpu.VMEM((height, 128), jnp.int32),
            pltpu.SemaphoreType.DMA((halos,)),
            pltpu.SemaphoreType.DMA((halos,)),
            pltpu.SemaphoreType.DMA((n,)),
            pltpu.SemaphoreType.DMA((n,)),
        ],
        compiler_params=pltpu.CompilerParams(collective_id=0, has_side_effects=True,
                                             vmem_limit_bytes=32 << 20),
        name="exchange",
    )(waveforms, tail, moveouts, station_count, bank_of_region)


def stack_kernel(taps, piece, scale, lists_ref, scal_ref, rec_ref, lib_hbm, mov_ref, out_ref,
                 lib_ref, hank0, hank1, fans, gain, pairs, place, lib_sem):
    comps, stations, record = rec_ref.shape
    slots, regions = lists_ref.shape
    channels = slots * comps
    templates = lib_ref.shape[1]
    moves = (record - piece - taps) // UNIT + 1
    width = piece + (moves - 1) * UNIT
    deep = 2 * UNIT
    reach = width + taps - deep
    rows = comps * stations

    lib_copy = pltpu.make_async_copy(lib_hbm, lib_ref, lib_sem)
    lib_copy.start()

    @pl.loop(0, stations + 1)
    def _(s):
        place[s] = 0

    @pl.loop(0, regions)
    def _(r):
        @pl.loop(0, scal_ref[r, 0])
        def _(k):
            s = lists_ref[k, r]
            place[s + 1] = place[s + 1] + 1

    @pl.loop(0, stations)
    def _(s):
        place[s + 1] = place[s + 1] + place[s]

    @pl.loop(0, regions)
    def _(r):
        @pl.loop(0, scal_ref[r, 0])
        def _(k):
            s = lists_ref[k, r]
            pairs[place[s]] = r * slots + k
            place[s] = place[s] + 1

    @pl.loop(0, stations, step=16)
    def _(s):
        s = pl.multiple_of(s, 16)
        for c in range(comps):
            x = rec_ref[c, pl.ds(s, 16)].astype(jnp.float32)
            for k in range(8):
                at = pl.multiple_of(k * rows + c * stations + s, 16)
                moved = pltpu.roll(x, record - k, 1) if k else x
                for j in range(fans.shape[0]):
                    fans[j, pl.ds(at, 16)] = moved[:, j * UNIT:(j + 1) * UNIT]
            window = x * x
            span = 1
            while span < taps:
                window = window + pltpu.roll(window, record - span, 1)
                span *= 2
            at = pl.multiple_of(c * stations + s, 16)
            gain[pl.ds(at, 16)] = lax.rsqrt(window[:, 0:width] / taps + 1e-05) * scale

    out_ref[...] = jnp.zeros_like(out_ref)
    diagonal = (lax.broadcasted_iota(jnp.int32, (templates, UNIT), 0)
                == lax.broadcasted_iota(jnp.int32, (templates, UNIT), 1))

    def build(s, hank):
        for c in range(comps):
            fan = jnp.concatenate([fans[j, pl.ds(c * stations + s, 8, stride=rows)]
                                   for j in range(fans.shape[0])], axis=1)
            fan = jnp.concatenate([fan, pltpu.roll(fan, record - 8, 1)], axis=0).astype(jnp.bfloat16)
            for g in range(0, UNIT, 16):
                both = (pltpu.roll(fan, record - g, 1) if g else fan).astype(jnp.bfloat16)
                hank[c, g:g + 16] = both[:, 0:reach]
                hank[c, UNIT + g:UNIT + g + 16] = both[:, UNIT:UNIT + reach]

    def chunk(s, first, end, hank):
        picks = []
        for p in range(PAIRS):
            at = jnp.maximum(jnp.minimum(first + p, end - 1), 0)
            pair = pairs[at]
            r = pair // slots
            channel = (pair - r * slots) * comps
            picks.append((r, scal_ref[r, 1] * channels + channel, channel,
                          jnp.where(first + p < end, 0, moves)))
        total = jnp.zeros(out_ref.shape, jnp.float32)
        for c in range(comps):
            kernels = jnp.concatenate([lib_ref[base + c] for _, base, _, _ in picks], axis=0)
            corr = None
            for d in range(taps // deep):
                term = jnp.dot(kernels[:, d * deep:(d + 1) * deep],
                               hank[c, :, d * deep:d * deep + width],
                               preferred_element_type=jnp.float32)
                corr = term if corr is None else corr + term
            corr = corr * gain[pl.ds(c * stations + s, 1)]
            for p, (r, _, channel, dead) in enumerate(picks):
                mine = corr[p * templates:(p + 1) * templates]
                delays = jnp.broadcast_to(mov_ref[r, pl.ds(channel + c, 1)], diagonal.shape)
                shift = jnp.sum(jnp.where(diagonal, delays, 0), axis=1, keepdims=True) + dead
                for m in range(moves):
                    total = total + jnp.where(shift == m, mine[:, m * UNIT:m * UNIT + piece], 0.0)
        return total

    def process(s, hank, other):
        end = place[s]
        begin = jnp.where(s == 0, 0, place[jnp.maximum(s - 1, 0)])
        total = chunk(s, begin, end, hank)
        build(jnp.minimum(s + 1, stations - 1), other)
        out_ref[...] += total

        @pl.loop(1, pl.cdiv(end - begin, PAIRS))
        def _(q):
            out_ref[...] += chunk(s, begin + q * PAIRS, end, hank)

    build(0, hank0)
    lib_copy.wait()

    @pl.loop(0, stations, step=2)
    def _(s):
        process(s, hank0, hank1)
        process(s + 1, hank1, hank0)


def stack(taps, piece, scale, lists, scal, record, bank_rows, meta):
    slots, regions = lists.shape
    comps, stations, samples = record.shape
    templates = bank_rows.shape[1]
    width = samples - taps
    vmem = pl.BlockSpec(memory_space=pltpu.VMEM)
    smem = pl.BlockSpec(memory_space=pltpu.SMEM)
    signal = pltpu.VMEM((comps, 2 * UNIT, width + taps - 2 * UNIT), jnp.bfloat16)
    return pl.pallas_call(
        functools.partial(stack_kernel, taps, piece, scale),
        out_shape=jax.ShapeDtypeStruct((templates, piece), jnp.float32),
        in_specs=[smem, smem, vmem, pl.BlockSpec(memory_space=pltpu.HBM), vmem],
        out_specs=vmem,
        scratch_shapes=[
            pltpu.VMEM(bank_rows.shape, bank_rows.dtype),
            signal,
            signal,
            pltpu.VMEM((samples // UNIT, 8 * comps * stations, UNIT), jnp.float32),
            pltpu.VMEM((comps * stations, width), jnp.float32),
            pltpu.SMEM((regions * slots,), jnp.int32),
            pltpu.SMEM((stations + 1,), jnp.int32),
            pltpu.SemaphoreType.DMA,
        ],
        compiler_params=pltpu.CompilerParams(vmem_limit_bytes=40 << 20),
        name="stack",
    )(lists, scal, record, bank_rows, meta)


def on_device(waveforms, tail, station_lists, station_count, bank_of_region, library, moveouts):
    regions = lax.axis_size("reg")
    comps, piece = waveforms.shape[1:]
    banks, templates, channels, taps = library.shape
    slots = station_lists.shape[1]
    scale = 1.0 / math.sqrt(comps * slots * regions)
    bank_rows = jnp.transpose(library, (0, 2, 1, 3)).reshape(banks * channels, templates, taps)
    record, meta = exchange(regions, jnp.transpose(waveforms, (1, 0, 2)), jnp.transpose(tail, (1, 0, 2)),
                            jnp.transpose(moveouts, (2, 0, 1)), station_count, bank_of_region)
    scal = meta[:, channels:channels + 2, 0]
    return stack(taps, piece, scale, station_lists.T, scal, record, bank_rows, meta)


def solution(mesh):
    return jax.shard_map(
        on_device,
        mesh=mesh,
        in_specs=(
            P("grp", None, "reg"),
            P("grp", None, None),
            P("grp", None),
            P(("grp", "reg")),
            P(("grp", "reg")),
            P(),
            P(("grp", "reg"), None, None),
        ),
        out_specs=P("grp", "reg"),
        check_vma=False,
    )
```

```python
import functools
import math

import jax
import jax.numpy as jnp
from jax import lax
from jax.experimental import pallas as pl
from jax.experimental.pallas import tpu as pltpu
from jax.sharding import PartitionSpec as P

UNIT = 128
PAIRS = 8


def exchange_kernel(n, wave_ref, tail_ref, mov_ref, count_ref, bank_ref, rec_ref, meta_ref,
                    mine, halo_send, halo_recv, meta_send, meta_recv):
    me = lax.axis_index("reg")
    piece = wave_ref.shape[2]
    halos = tail_ref.shape[2] // piece
    channels, _, templates = mov_ref.shape

    mine[...] = jnp.zeros_like(mine)
    for c in range(channels):
        mine[c:c + 1, 0:templates] = mov_ref[c]
    mine[channels:channels + 1] = jnp.full((1, mine.shape[1]), count_ref[0], jnp.int32)
    mine[channels + 1:channels + 2] = jnp.full((1, mine.shape[1]), bank_ref[0], jnp.int32)

    barrier = pltpu.get_barrier_semaphore()

    @pl.loop(1, n)
    def _(step):
        pl.semaphore_signal(barrier, inc=1, device_id={"reg": lax.rem(me + step, n)},
                            device_id_type=pl.DeviceIdType.MESH)

    pl.semaphore_wait(barrier, n - 1)

    def halo_copy(h):
        return pltpu.make_async_remote_copy(
            src_ref=wave_ref,
            dst_ref=rec_ref.at[:, :, pl.ds(h * piece, piece)],
            send_sem=halo_send.at[h - 1],
            recv_sem=halo_recv.at[h - 1],
            device_id={"reg": lax.rem(me + n - h, n)},
            device_id_type=pl.DeviceIdType.MESH,
        )

    for h in range(1, halos + 1):
        @pl.when(me >= h)
        def _():
            halo_copy(h).start()

    def meta_copy(step):
        return pltpu.make_async_remote_copy(
            src_ref=mine,
            dst_ref=meta_ref.at[me],
            send_sem=meta_send.at[step],
            recv_sem=meta_recv.at[step],
            device_id={"reg": lax.rem(me + step, n)},
            device_id_type=pl.DeviceIdType.MESH,
        )

    @pl.loop(1, n)
    def _(step):
        meta_copy(step).start()

    meta_ref[me] = mine[...]
    rec_ref[:, :, 0:piece] = wave_ref[...]
    for h in range(1, halos + 1):
        for q in range(h):
            @pl.when(me + h - n == q)
            def _():
                rec_ref[:, :, h * piece:(h + 1) * piece] = tail_ref[:, :, q * piece:(q + 1) * piece]

    for h in range(1, halos + 1):
        @pl.when(me >= h)
        def _():
            halo_copy(h).wait_send()

        @pl.when(me + h < n)
        def _():
            halo_copy(h).wait_recv()

    @pl.loop(1, n)
    def _(step):
        meta_copy(step).wait_send()
        meta_copy(step).wait_recv()


def exchange(n, waveforms, tail, moveouts, station_count, bank_of_region):
    comps, stations, piece = waveforms.shape
    height = -(-(moveouts.shape[0] + 2) // 8) * 8
    halos = tail.shape[2] // piece
    vmem = pl.BlockSpec(memory_space=pltpu.VMEM)
    smem = pl.BlockSpec(memory_space=pltpu.SMEM)
    return pl.pallas_call(
        functools.partial(exchange_kernel, n),
        out_shape=(
            jax.ShapeDtypeStruct((comps, stations, piece + tail.shape[2]), waveforms.dtype),
            jax.ShapeDtypeStruct((n, height, 128), jnp.int32),
        ),
        in_specs=[vmem, vmem, vmem, smem, smem],
        out_specs=(vmem, vmem),
        scratch_shapes=[
            pltpu.VMEM((height, 128), jnp.int32),
            pltpu.SemaphoreType.DMA((halos,)),
            pltpu.SemaphoreType.DMA((halos,)),
            pltpu.SemaphoreType.DMA((n,)),
            pltpu.SemaphoreType.DMA((n,)),
        ],
        compiler_params=pltpu.CompilerParams(collective_id=0, has_side_effects=True,
                                             vmem_limit_bytes=62 << 20),
        name="exchange",
    )(waveforms, tail, moveouts, station_count, bank_of_region)


def stack_kernel(taps, piece, scale, lists_ref, scal_ref, rec_ref, lib_hbm, mov_ref, out_ref,
                 lib_ref, hank0, hank1, fans, gain, pairs, place, lib_sem):
    comps, stations, record = rec_ref.shape
    slots, regions = lists_ref.shape
    channels = slots * comps
    templates = lib_ref.shape[1]
    moves = (record - piece - taps) // UNIT + 1
    width = piece + (moves - 1) * UNIT
    deep = 2 * UNIT
    reach = width + taps - deep
    rows = comps * stations

    lib_copy = pltpu.make_async_copy(lib_hbm, lib_ref, lib_sem)
    lib_copy.start()

    @pl.loop(0, stations + 1)
    def _(s):
        place[s] = 0

    @pl.loop(0, regions)
    def _(r):
        @pl.loop(0, scal_ref[r, 0])
        def _(k):
            s = lists_ref[k, r]
            place[s + 1] = place[s + 1] + 1

    @pl.loop(0, stations)
    def _(s):
        place[s + 1] = place[s + 1] + place[s]

    @pl.loop(0, regions)
    def _(r):
        @pl.loop(0, scal_ref[r, 0])
        def _(k):
            s = lists_ref[k, r]
            pairs[place[s]] = r * slots + k
            place[s] = place[s] + 1

    @pl.loop(0, stations, step=16)
    def _(s):
        s = pl.multiple_of(s, 16)
        for c in range(comps):
            x = rec_ref[c, pl.ds(s, 16)].astype(jnp.float32)
            for k in range(8):
                at = pl.multiple_of(k * rows + c * stations + s, 16)
                moved = pltpu.roll(x, record - k, 1) if k else x
                for j in range(fans.shape[0]):
                    fans[j, pl.ds(at, 16)] = moved[:, j * UNIT:(j + 1) * UNIT]
            window = x * x
            span = 1
            while span < taps:
                window = window + pltpu.roll(window, record - span, 1)
                span *= 2
            at = pl.multiple_of(c * stations + s, 16)
            gain[pl.ds(at, 16)] = lax.rsqrt(window[:, 0:width] / taps + 1e-05) * scale

    out_ref[...] = jnp.zeros_like(out_ref)
    diagonal = (lax.broadcasted_iota(jnp.int32, (templates, UNIT), 0)
                == lax.broadcasted_iota(jnp.int32, (templates, UNIT), 1))

    def build(s, hank):
        for c in range(comps):
            fan = jnp.concatenate([fans[j, pl.ds(c * stations + s, 8, stride=rows)]
                                   for j in range(fans.shape[0])], axis=1)
            fan = jnp.concatenate([fan, pltpu.roll(fan, record - 8, 1)], axis=0).astype(jnp.bfloat16)
            for g in range(0, UNIT, 16):
                both = (pltpu.roll(fan, record - g, 1) if g else fan).astype(jnp.bfloat16)
                hank[c, g:g + 16] = both[:, 0:reach]
                hank[c, UNIT + g:UNIT + g + 16] = both[:, UNIT:UNIT + reach]

    def chunk(s, first, end, hank):
        picks = []
        for p in range(PAIRS):
            at = jnp.maximum(jnp.minimum(first + p, end - 1), 0)
            pair = pairs[at]
            r = pair // slots
            channel = (pair - r * slots) * comps
            picks.append((r, scal_ref[r, 1] * channels + channel, channel,
                          jnp.where(first + p < end, 0, moves)))
        total = jnp.zeros(out_ref.shape, jnp.float32)
        for c in range(comps):
            kernels = jnp.concatenate([lib_ref[base + c] for _, base, _, _ in picks], axis=0)
            corr = None
            for d in range(taps // deep):
                term = jnp.dot(kernels[:, d * deep:(d + 1) * deep],
                               hank[c, :, d * deep:d * deep + width],
                               preferred_element_type=jnp.float32)
                corr = term if corr is None else corr + term
            corr = corr * gain[pl.ds(c * stations + s, 1)]
            for p, (r, _, channel, dead) in enumerate(picks):
                mine = corr[p * templates:(p + 1) * templates]
                delays = jnp.broadcast_to(mov_ref[r, pl.ds(channel + c, 1)], diagonal.shape)
                shift = jnp.sum(jnp.where(diagonal, delays, 0), axis=1, keepdims=True) + dead
                for m in range(moves):
                    total = total + jnp.where(shift == m, mine[:, m * UNIT:m * UNIT + piece], 0.0)
        return total

    def process(s, hank, other):
        end = place[s]
        begin = jnp.where(s == 0, 0, place[jnp.maximum(s - 1, 0)])
        total = chunk(s, begin, end, hank)
        build(jnp.minimum(s + 1, stations - 1), other)
        out_ref[...] += total

        @pl.loop(1, pl.cdiv(end - begin, PAIRS))
        def _(q):
            out_ref[...] += chunk(s, begin + q * PAIRS, end, hank)

    build(0, hank0)
    lib_copy.wait()

    @pl.loop(0, stations, step=2)
    def _(s):
        process(s, hank0, hank1)
        process(s + 1, hank1, hank0)


def stack(taps, piece, scale, lists, scal, record, bank_rows, meta):
    slots, regions = lists.shape
    comps, stations, samples = record.shape
    templates = bank_rows.shape[1]
    width = samples - taps
    vmem = pl.BlockSpec(memory_space=pltpu.VMEM)
    smem = pl.BlockSpec(memory_space=pltpu.SMEM)
    signal = pltpu.VMEM((comps, 2 * UNIT, width + taps - 2 * UNIT), jnp.bfloat16)
    return pl.pallas_call(
        functools.partial(stack_kernel, taps, piece, scale),
        out_shape=jax.ShapeDtypeStruct((templates, piece), jnp.float32),
        in_specs=[smem, smem, vmem, pl.BlockSpec(memory_space=pl.ANY), vmem],
        out_specs=vmem,
        scratch_shapes=[
            pltpu.VMEM(bank_rows.shape, bank_rows.dtype),
            signal,
            signal,
            pltpu.VMEM((samples // UNIT, 8 * comps * stations, UNIT), jnp.float32),
            pltpu.VMEM((comps * stations, width), jnp.float32),
            pltpu.SMEM((regions * slots,), jnp.int32),
            pltpu.SMEM((stations + 1,), jnp.int32),
            pltpu.SemaphoreType.DMA,
        ],
        compiler_params=pltpu.CompilerParams(vmem_limit_bytes=62 << 20),
        name="stack",
    )(lists, scal, record, bank_rows, meta)


def on_device(waveforms, tail, station_lists, station_count, bank_of_region, library, moveouts):
    regions = lax.axis_size("reg")
    comps, piece = waveforms.shape[1:]
    banks, templates, channels, taps = library.shape
    slots = station_lists.shape[1]
    scale = 1.0 / math.sqrt(comps * slots * regions)
    bank_rows = jnp.transpose(library, (0, 2, 1, 3)).reshape(banks * channels, templates, taps)
    record, meta = exchange(regions, jnp.transpose(waveforms, (1, 0, 2)), jnp.transpose(tail, (1, 0, 2)),
                            jnp.transpose(moveouts, (2, 0, 1)), station_count, bank_of_region)
    scal = meta[:, channels:channels + 2, 0]
    return stack(taps, piece, scale, station_lists.T, scal, record, bank_rows, meta)


def solution(mesh):
    return jax.shard_map(
        on_device,
        mesh=mesh,
        in_specs=(
            P("grp", None, "reg"),
            P("grp", None, None),
            P("grp", None),
            P(("grp", "reg")),
            P(("grp", "reg")),
            P(),
            P(("grp", "reg"), None, None),
        ),
        out_specs=P("grp", "reg"),
        check_vma=False,
    )
```

```python
import functools
import math

import jax
import jax.numpy as jnp
from jax import lax
from jax.experimental import pallas as pl
from jax.experimental.pallas import tpu as pltpu
from jax.sharding import PartitionSpec as P

UNIT = 128
PAIRS = 8


def exchange_kernel(n, wave_ref, tail_ref, mov_ref, count_ref, bank_ref, rec_ref, meta_ref,
                    mine, halo_send, halo_recv, meta_send, meta_recv):
    me = lax.axis_index("reg")
    piece = wave_ref.shape[2]
    halos = tail_ref.shape[2] // piece
    channels, _, templates = mov_ref.shape

    mine[...] = jnp.zeros_like(mine)
    for c in range(channels):
        mine[c:c + 1, 0:templates] = mov_ref[c]
    mine[channels:channels + 1] = jnp.full((1, mine.shape[1]), count_ref[0], jnp.int32)
    mine[channels + 1:channels + 2] = jnp.full((1, mine.shape[1]), bank_ref[0], jnp.int32)

    barrier = pltpu.get_barrier_semaphore()

    @pl.loop(1, n)
    def _(step):
        pl.semaphore_signal(barrier, inc=1, device_id={"reg": lax.rem(me + step, n)},
                            device_id_type=pl.DeviceIdType.MESH)

    pl.semaphore_wait(barrier, n - 1)

    def halo_copy(h):
        return pltpu.make_async_remote_copy(
            src_ref=wave_ref,
            dst_ref=rec_ref.at[:, :, pl.ds(h * piece, piece)],
            send_sem=halo_send.at[h - 1],
            recv_sem=halo_recv.at[h - 1],
            device_id={"reg": lax.rem(me + n - h, n)},
            device_id_type=pl.DeviceIdType.MESH,
        )

    for h in range(1, halos + 1):
        @pl.when(me >= h)
        def _():
            halo_copy(h).start()

    def meta_copy(step):
        return pltpu.make_async_remote_copy(
            src_ref=mine,
            dst_ref=meta_ref.at[me],
            send_sem=meta_send.at[step],
            recv_sem=meta_recv.at[step],
            device_id={"reg": lax.rem(me + step, n)},
            device_id_type=pl.DeviceIdType.MESH,
        )

    @pl.loop(1, n)
    def _(step):
        meta_copy(step).start()

    meta_ref[me] = mine[...]
    rec_ref[:, :, 0:piece] = wave_ref[...]
    for h in range(1, halos + 1):
        for q in range(h):
            @pl.when(me + h - n == q)
            def _():
                rec_ref[:, :, h * piece:(h + 1) * piece] = tail_ref[:, :, q * piece:(q + 1) * piece]

    for h in range(1, halos + 1):
        @pl.when(me >= h)
        def _():
            halo_copy(h).wait_send()

        @pl.when(me + h < n)
        def _():
            halo_copy(h).wait_recv()

    @pl.loop(1, n)
    def _(step):
        meta_copy(step).wait_send()
        meta_copy(step).wait_recv()


def exchange(n, waveforms, tail, moveouts, station_count, bank_of_region):
    comps, stations, piece = waveforms.shape
    height = -(-(moveouts.shape[0] + 2) // 8) * 8
    halos = tail.shape[2] // piece
    vmem = pl.BlockSpec(memory_space=pltpu.VMEM)
    smem = pl.BlockSpec(memory_space=pltpu.SMEM)
    return pl.pallas_call(
        functools.partial(exchange_kernel, n),
        out_shape=(
            jax.ShapeDtypeStruct((comps, stations, piece + tail.shape[2]), waveforms.dtype),
            jax.ShapeDtypeStruct((n, height, 128), jnp.int32),
        ),
        in_specs=[vmem, vmem, vmem, smem, smem],
        out_specs=(vmem, vmem),
        scratch_shapes=[
            pltpu.VMEM((height, 128), jnp.int32),
            pltpu.SemaphoreType.DMA((halos,)),
            pltpu.SemaphoreType.DMA((halos,)),
            pltpu.SemaphoreType.DMA((n,)),
            pltpu.SemaphoreType.DMA((n,)),
        ],
        compiler_params=pltpu.CompilerParams(collective_id=0, has_side_effects=True,
                                             vmem_limit_bytes=62 << 20),
        name="exchange",
    )(waveforms, tail, moveouts, station_count, bank_of_region)


def stack_kernel(taps, piece, scale, lists_ref, rec_ref, lib_hbm, mov_ref, out_ref,
                 lib_ref, hank0, hank1, fans, gain, pairs, place, scal_ref, lib_sem, scal_sem):
    comps, stations, record = rec_ref.shape
    slots, regions = lists_ref.shape
    channels = slots * comps
    templates = lib_ref.shape[1]
    moves = (record - piece - taps) // UNIT + 1
    width = piece + (moves - 1) * UNIT
    deep = 2 * UNIT
    reach = width + taps - deep
    rows = comps * stations

    lib_copy = pltpu.make_async_copy(lib_hbm, lib_ref, lib_sem)
    lib_copy.start()
    facts = channels // 8 * 8
    scal_copy = pltpu.make_async_copy(mov_ref.at[:, facts:facts + 8, :], scal_ref, scal_sem)

    scal_copy.start()

    @pl.loop(0, stations, step=16)
    def _(s):
        s = pl.multiple_of(s, 16)
        for c in range(comps):
            x = rec_ref[c, pl.ds(s, 16)].astype(jnp.float32)
            for k in range(8):
                at = pl.multiple_of(k * rows + c * stations + s, 16)
                moved = pltpu.roll(x, record - k, 1) if k else x
                for j in range(fans.shape[0]):
                    fans[j, pl.ds(at, 16)] = moved[:, j * UNIT:(j + 1) * UNIT]
            window = x * x
            span = 1
            while span < taps:
                window = window + pltpu.roll(window, record - span, 1)
                span *= 2
            at = pl.multiple_of(c * stations + s, 16)
            gain[pl.ds(at, 16)] = lax.rsqrt(window[:, 0:width] / taps + 1e-05) * scale

    scal_copy.wait()
    for s in range(stations + 1):
        place[s] = 0

    @pl.loop(0, regions)
    def _(r):
        count = scal_ref[r, channels - facts, 0]
        for k in range(slots):
            s = lists_ref[k, r]
            place[s + 1] = place[s + 1] + jnp.where(k < count, 1, 0)

    @pl.loop(0, stations)
    def _(s):
        place[s + 1] = place[s + 1] + place[s]

    @pl.loop(0, regions)
    def _(r):
        count = scal_ref[r, channels - facts, 0]
        for k in range(slots):
            s = lists_ref[k, r]
            at = place[s]
            live = k < count
            pairs[jnp.where(live, at, regions * slots)] = r * slots + k
            place[s] = at + jnp.where(live, 1, 0)

    out_ref[...] = jnp.zeros_like(out_ref)
    diagonal = (lax.broadcasted_iota(jnp.int32, (templates, UNIT), 0)
                == lax.broadcasted_iota(jnp.int32, (templates, UNIT), 1))

    def build(s, hank):
        for c in range(comps):
            fan = jnp.concatenate([fans[j, pl.ds(c * stations + s, 8, stride=rows)]
                                   for j in range(fans.shape[0])], axis=1)
            fan = jnp.concatenate([fan, pltpu.roll(fan, record - 8, 1)], axis=0).astype(jnp.bfloat16)
            for g in range(0, UNIT, 16):
                both = (pltpu.roll(fan, record - g, 1) if g else fan).astype(jnp.bfloat16)
                hank[c, g:g + 16] = both[:, 0:reach]
                hank[c, UNIT + g:UNIT + g + 16] = both[:, UNIT:UNIT + reach]

    def chunk(s, first, end, hank):
        picks = []
        for p in range(PAIRS):
            at = jnp.maximum(jnp.minimum(first + p, end - 1), 0)
            pair = pairs[at]
            r = pair // slots
            channel = (pair - r * slots) * comps
            picks.append((r, scal_ref[r, channels - facts + 1, 0] * channels + channel, channel,
                          jnp.where(first + p < end, 0, moves)))
        total = jnp.zeros(out_ref.shape, jnp.float32)
        for c in range(comps):
            kernels = jnp.concatenate([lib_ref[base + c] for _, base, _, _ in picks], axis=0)
            corr = None
            for d in range(taps // deep):
                term = jnp.dot(kernels[:, d * deep:(d + 1) * deep],
                               hank[c, :, d * deep:d * deep + width],
                               preferred_element_type=jnp.float32)
                corr = term if corr is None else corr + term
            corr = corr * gain[pl.ds(c * stations + s, 1)]
            for p, (r, _, channel, dead) in enumerate(picks):
                mine = corr[p * templates:(p + 1) * templates]
                delays = jnp.broadcast_to(mov_ref[r, pl.ds(channel + c, 1)], diagonal.shape)
                shift = jnp.sum(jnp.where(diagonal, delays, 0), axis=1, keepdims=True) + dead
                for m in range(moves):
                    total = total + jnp.where(shift == m, mine[:, m * UNIT:m * UNIT + piece], 0.0)
        return total

    def process(s, hank, other):
        end = place[s]
        begin = jnp.where(s == 0, 0, place[jnp.maximum(s - 1, 0)])
        total = chunk(s, begin, end, hank)
        build(jnp.minimum(s + 1, stations - 1), other)
        out_ref[...] += total

        @pl.loop(1, pl.cdiv(end - begin, PAIRS))
        def _(q):
            out_ref[...] += chunk(s, begin + q * PAIRS, end, hank)

    build(0, hank0)
    lib_copy.wait()

    @pl.loop(0, stations, step=2)
    def _(s):
        process(s, hank0, hank1)
        process(s + 1, hank1, hank0)


def stack(taps, piece, scale, lists, record, bank_rows, meta):
    slots, regions = lists.shape
    comps, stations, samples = record.shape
    templates = bank_rows.shape[1]
    width = samples - taps
    vmem = pl.BlockSpec(memory_space=pltpu.VMEM)
    smem = pl.BlockSpec(memory_space=pltpu.SMEM)
    signal = pltpu.VMEM((comps, 2 * UNIT, width + taps - 2 * UNIT), jnp.bfloat16)
    return pl.pallas_call(
        functools.partial(stack_kernel, taps, piece, scale),
        out_shape=jax.ShapeDtypeStruct((templates, piece), jnp.float32),
        in_specs=[smem, vmem, pl.BlockSpec(memory_space=pl.ANY), vmem],
        out_specs=vmem,
        scratch_shapes=[
            pltpu.VMEM(bank_rows.shape, bank_rows.dtype),
            signal,
            signal,
            pltpu.VMEM((samples // UNIT, 8 * comps * stations, UNIT), jnp.float32),
            pltpu.VMEM((comps * stations, width), jnp.float32),
            pltpu.SMEM((regions * slots + 1,), jnp.int32),
            pltpu.SMEM((stations + 1,), jnp.int32),
            pltpu.SMEM((regions, 8, meta.shape[2]), jnp.int32),
            pltpu.SemaphoreType.DMA,
            pltpu.SemaphoreType.DMA,
        ],
        compiler_params=pltpu.CompilerParams(vmem_limit_bytes=62 << 20),
        name="stack",
    )(lists, record, bank_rows, meta)


def on_device(waveforms, tail, station_lists, station_count, bank_of_region, library, moveouts):
    regions = lax.axis_size("reg")
    comps, piece = waveforms.shape[1:]
    banks, templates, channels, taps = library.shape
    slots = station_lists.shape[1]
    scale = 1.0 / math.sqrt(comps * slots * regions)
    bank_rows = jnp.transpose(library, (0, 2, 1, 3)).reshape(banks * channels, templates, taps)
    record, meta = exchange(regions, jnp.transpose(waveforms, (1, 0, 2)), jnp.transpose(tail, (1, 0, 2)),
                            jnp.transpose(moveouts, (2, 0, 1)), station_count, bank_of_region)
    return stack(taps, piece, scale, station_lists.T, record, bank_rows, meta)


def solution(mesh):
    return jax.shard_map(
        on_device,
        mesh=mesh,
        in_specs=(
            P("grp", None, "reg"),
            P("grp", None, None),
            P("grp", None),
            P(("grp", "reg")),
            P(("grp", "reg")),
            P(),
            P(("grp", "reg"), None, None),
        ),
        out_specs=P("grp", "reg"),
        check_vma=False,
    )
```

```python
import functools
import math

import jax
import jax.numpy as jnp
from jax import lax
from jax.experimental import pallas as pl
from jax.experimental.pallas import tpu as pltpu
from jax.sharding import PartitionSpec as P

UNIT = 128
PAIRS = 8


def exchange_kernel(n, wave_ref, tail_ref, mov_ref, count_ref, bank_ref, rec_ref, meta_ref,
                    mine, local, halo_send, halo_recv, meta_send, meta_recv):
    me = lax.axis_index("reg")
    piece = wave_ref.shape[2]
    halos = tail_ref.shape[2] // piece
    channels, _, templates = mov_ref.shape

    mine[...] = jnp.zeros_like(mine)
    for c in range(channels):
        mine[c:c + 1, 0:templates] = mov_ref[c]
    mine[channels:channels + 1] = jnp.full((1, mine.shape[1]), count_ref[0], jnp.int32)
    mine[channels + 1:channels + 2] = jnp.full((1, mine.shape[1]), bank_ref[0], jnp.int32)

    own_copies = [
        pltpu.make_async_copy(wave_ref, rec_ref.at[:, :, pl.ds(0, piece)], local.at[0]),
        pltpu.make_async_copy(mine, meta_ref.at[me], local.at[1]),
    ]

    def tail_copy(h, q):
        return pltpu.make_async_copy(tail_ref.at[:, :, pl.ds(q * piece, piece)],
                                     rec_ref.at[:, :, pl.ds(h * piece, piece)], local.at[h + 1])

    for copy in own_copies:
        copy.start()
    for h in range(1, halos + 1):
        for q in range(h):
            @pl.when(me + h - n == q)
            def _():
                tail_copy(h, q).start()

    barrier = pltpu.get_barrier_semaphore()

    @pl.loop(1, n)
    def _(step):
        pl.semaphore_signal(barrier, inc=1, device_id={"reg": lax.rem(me + step, n)},
                            device_id_type=pl.DeviceIdType.MESH)

    pl.semaphore_wait(barrier, n - 1)

    def halo_copy(h):
        return pltpu.make_async_remote_copy(
            src_ref=wave_ref,
            dst_ref=rec_ref.at[:, :, pl.ds(h * piece, piece)],
            send_sem=halo_send.at[h - 1],
            recv_sem=halo_recv.at[h - 1],
            device_id={"reg": lax.rem(me + n - h, n)},
            device_id_type=pl.DeviceIdType.MESH,
        )

    for h in range(1, halos + 1):
        @pl.when(me >= h)
        def _():
            halo_copy(h).start()

    def meta_copy(step):
        return pltpu.make_async_remote_copy(
            src_ref=mine,
            dst_ref=meta_ref.at[me],
            send_sem=meta_send.at[step],
            recv_sem=meta_recv.at[step],
            device_id={"reg": lax.rem(me + step, n)},
            device_id_type=pl.DeviceIdType.MESH,
        )

    @pl.loop(1, n)
    def _(step):
        meta_copy(step).start()

    for copy in own_copies:
        copy.wait()
    for h in range(1, halos + 1):
        for q in range(h):
            @pl.when(me + h - n == q)
            def _():
                tail_copy(h, q).wait()

        @pl.when(me >= h)
        def _():
            halo_copy(h).wait_send()

        @pl.when(me + h < n)
        def _():
            halo_copy(h).wait_recv()

    @pl.loop(1, n)
    def _(step):
        meta_copy(step).wait_send()
        meta_copy(step).wait_recv()


def exchange(n, waveforms, tail, moveouts, station_count, bank_of_region):
    comps, stations, piece = waveforms.shape
    height = -(-(moveouts.shape[0] + 2) // 8) * 8
    halos = tail.shape[2] // piece
    vmem = pl.BlockSpec(memory_space=pltpu.VMEM)
    anywhere = pl.BlockSpec(memory_space=pl.ANY)
    smem = pl.BlockSpec(memory_space=pltpu.SMEM)
    return pl.pallas_call(
        functools.partial(exchange_kernel, n),
        out_shape=(
            jax.ShapeDtypeStruct((comps, stations, piece + tail.shape[2]), waveforms.dtype),
            jax.ShapeDtypeStruct((n, height, 128), jnp.int32),
        ),
        in_specs=[anywhere, anywhere, vmem, smem, smem],
        out_specs=(anywhere, anywhere),
        scratch_shapes=[
            pltpu.VMEM((height, 128), jnp.int32),
            pltpu.SemaphoreType.DMA((halos + 2,)),
            pltpu.SemaphoreType.DMA((halos,)),
            pltpu.SemaphoreType.DMA((halos,)),
            pltpu.SemaphoreType.DMA((n,)),
            pltpu.SemaphoreType.DMA((n,)),
        ],
        compiler_params=pltpu.CompilerParams(collective_id=0, has_side_effects=True,
                                             vmem_limit_bytes=62 << 20),
        name="exchange",
    )(waveforms, tail, moveouts, station_count, bank_of_region)


def stack_kernel(taps, piece, scale, lists_ref, rec_ref, lib_hbm, mov_ref, out_ref,
                 lib_ref, hank0, hank1, fans, gain, pairs, place, scal_ref, lib_sem, scal_sem):
    comps, stations, record = rec_ref.shape
    slots, regions = lists_ref.shape
    channels = slots * comps
    templates = lib_ref.shape[1]
    moves = (record - piece - taps) // UNIT + 1
    width = piece + (moves - 1) * UNIT
    deep = 2 * UNIT
    reach = width + taps - deep
    rows = comps * stations

    lib_copy = pltpu.make_async_copy(lib_hbm, lib_ref, lib_sem)
    lib_copy.start()
    facts = channels // 8 * 8
    scal_copy = pltpu.make_async_copy(mov_ref.at[:, facts:facts + 8, :], scal_ref, scal_sem)

    scal_copy.start()

    @pl.loop(0, stations, step=16)
    def _(s):
        s = pl.multiple_of(s, 16)
        for c in range(comps):
            x = rec_ref[c, pl.ds(s, 16)].astype(jnp.float32)
            for k in range(8):
                at = pl.multiple_of(k * rows + c * stations + s, 16)
                moved = pltpu.roll(x, record - k, 1) if k else x
                for j in range(fans.shape[0]):
                    fans[j, pl.ds(at, 16)] = moved[:, j * UNIT:(j + 1) * UNIT]
            window = x * x
            span = 1
            while span < taps:
                window = window + pltpu.roll(window, record - span, 1)
                span *= 2
            at = pl.multiple_of(c * stations + s, 16)
            gain[pl.ds(at, 16)] = lax.rsqrt(window[:, 0:width] / taps + 1e-05) * scale

    scal_copy.wait()
    for s in range(stations + 1):
        place[s] = 0

    @pl.loop(0, regions)
    def _(r):
        count = scal_ref[r, channels - facts, 0]
        for k in range(slots):
            s = lists_ref[k, r]
            place[s + 1] = place[s + 1] + jnp.where(k < count, 1, 0)

    @pl.loop(0, stations)
    def _(s):
        place[s + 1] = place[s + 1] + place[s]

    @pl.loop(0, regions)
    def _(r):
        count = scal_ref[r, channels - facts, 0]
        for k in range(slots):
            s = lists_ref[k, r]
            at = place[s]
            live = k < count
            pairs[jnp.where(live, at, regions * slots)] = r * slots + k
            place[s] = at + jnp.where(live, 1, 0)

    out_ref[...] = jnp.zeros_like(out_ref)
    diagonal = (lax.broadcasted_iota(jnp.int32, (templates, UNIT), 0)
                == lax.broadcasted_iota(jnp.int32, (templates, UNIT), 1))

    def build(s, hank):
        for c in range(comps):
            fan = jnp.concatenate([fans[j, pl.ds(c * stations + s, 8, stride=rows)]
                                   for j in range(fans.shape[0])], axis=1)
            fan = jnp.concatenate([fan, pltpu.roll(fan, record - 8, 1)], axis=0).astype(jnp.bfloat16)
            for g in range(0, UNIT, 16):
                both = (pltpu.roll(fan, record - g, 1) if g else fan).astype(jnp.bfloat16)
                hank[c, g:g + 16] = both[:, 0:reach]
                hank[c, UNIT + g:UNIT + g + 16] = both[:, UNIT:UNIT + reach]

    def chunk(s, first, end, hank):
        picks = []
        for p in range(PAIRS):
            at = jnp.maximum(jnp.minimum(first + p, end - 1), 0)
            pair = pairs[at]
            r = pair // slots
            channel = (pair - r * slots) * comps
            picks.append((r, scal_ref[r, channels - facts + 1, 0] * channels + channel, channel,
                          jnp.where(first + p < end, 0, moves)))
        total = jnp.zeros(out_ref.shape, jnp.float32)
        for c in range(comps):
            kernels = jnp.concatenate([lib_ref[base + c] for _, base, _, _ in picks], axis=0)
            corr = None
            for d in range(taps // deep):
                term = jnp.dot(kernels[:, d * deep:(d + 1) * deep],
                               hank[c, :, d * deep:d * deep + width],
                               preferred_element_type=jnp.float32)
                corr = term if corr is None else corr + term
            corr = corr * gain[pl.ds(c * stations + s, 1)]
            for p, (r, _, channel, dead) in enumerate(picks):
                mine = corr[p * templates:(p + 1) * templates]
                delays = jnp.broadcast_to(mov_ref[r, pl.ds(channel + c, 1)], diagonal.shape)
                shift = jnp.sum(jnp.where(diagonal, delays, 0), axis=1, keepdims=True) + dead
                for m in range(moves):
                    total = total + jnp.where(shift == m, mine[:, m * UNIT:m * UNIT + piece], 0.0)
        return total

    def process(s, hank, other):
        end = place[s]
        begin = jnp.where(s == 0, 0, place[jnp.maximum(s - 1, 0)])
        total = chunk(s, begin, end, hank)
        build(jnp.minimum(s + 1, stations - 1), other)
        out_ref[...] += total

        @pl.loop(1, pl.cdiv(end - begin, PAIRS))
        def _(q):
            out_ref[...] += chunk(s, begin + q * PAIRS, end, hank)

    build(0, hank0)
    lib_copy.wait()

    @pl.loop(0, stations, step=2)
    def _(s):
        process(s, hank0, hank1)
        process(s + 1, hank1, hank0)


def stack(taps, piece, scale, lists, record, bank_rows, meta):
    slots, regions = lists.shape
    comps, stations, samples = record.shape
    templates = bank_rows.shape[1]
    width = samples - taps
    vmem = pl.BlockSpec(memory_space=pltpu.VMEM)
    smem = pl.BlockSpec(memory_space=pltpu.SMEM)
    signal = pltpu.VMEM((comps, 2 * UNIT, width + taps - 2 * UNIT), jnp.bfloat16)
    return pl.pallas_call(
        functools.partial(stack_kernel, taps, piece, scale),
        out_shape=jax.ShapeDtypeStruct((templates, piece), jnp.float32),
        in_specs=[smem, vmem, pl.BlockSpec(memory_space=pl.ANY), vmem],
        out_specs=vmem,
        scratch_shapes=[
            pltpu.VMEM(bank_rows.shape, bank_rows.dtype),
            signal,
            signal,
            pltpu.VMEM((samples // UNIT, 8 * comps * stations, UNIT), jnp.float32),
            pltpu.VMEM((comps * stations, width), jnp.float32),
            pltpu.SMEM((regions * slots + 1,), jnp.int32),
            pltpu.SMEM((stations + 1,), jnp.int32),
            pltpu.SMEM((regions, 8, meta.shape[2]), jnp.int32),
            pltpu.SemaphoreType.DMA,
            pltpu.SemaphoreType.DMA,
        ],
        compiler_params=pltpu.CompilerParams(vmem_limit_bytes=62 << 20),
        name="stack",
    )(lists, record, bank_rows, meta)


def on_device(waveforms, tail, station_lists, station_count, bank_of_region, library, moveouts):
    regions = lax.axis_size("reg")
    comps, piece = waveforms.shape[1:]
    banks, templates, channels, taps = library.shape
    slots = station_lists.shape[1]
    scale = 1.0 / math.sqrt(comps * slots * regions)
    bank_rows = jnp.transpose(library, (0, 2, 1, 3)).reshape(banks * channels, templates, taps)
    record, meta = exchange(regions, jnp.transpose(waveforms, (1, 0, 2)), jnp.transpose(tail, (1, 0, 2)),
                            jnp.transpose(moveouts, (2, 0, 1)), station_count, bank_of_region)
    return stack(taps, piece, scale, station_lists.T, record, bank_rows, meta)


def solution(mesh):
    return jax.shard_map(
        on_device,
        mesh=mesh,
        in_specs=(
            P("grp", None, "reg"),
            P("grp", None, None),
            P("grp", None),
            P(("grp", "reg")),
            P(("grp", "reg")),
            P(),
            P(("grp", "reg"), None, None),
        ),
        out_specs=P("grp", "reg"),
        check_vma=False,
    )
```
